32 devices in a mesh: dp: 4 (over y, core), seq: 8 (over z, x).
Axes of the slice: x: 2, y: 2, z: 4, core: 2. Of those that a mesh axis runs over, the one named last changes fastest.
Arguments:
- tokens: bfloat16 [4, 24, 256, 1280], P('dp', 'seq'), may hold values from -6 to 6
- clip_ids: int32 [4, 24], P('dp'), may hold values from 0 to 5, never falling along the last dimension, each value on 1 to 12 neighbouring positions
- ln_gain: float32 [1280], replicated, may hold values from 0.1 to 1.9
- w_qkv: bfloat16 [1280, 1920], P(None, 'dp'), may hold values from -0.15625 to 0.15625
- w_out: bfloat16 [640, 1280], P(None, 'dp'), may hold values from -0.25 to 0.25
Outputs:
- output: bfloat16 [4, 24, 256, 1280], P('dp', 'seq')
The draws below stay inside these ranges and needn't reach their ends.
Inputs may be any that keep to these rules, and one draw needn't show every extreme that they name: `clip_ids`: in each batch the clip numbers never fall along the frames, every clip number occurs, each clip covers 1 to 12 consecutive frames, and some clip covers exactly 12.
All inputs are finite; a program needn't handle non-finite values.
Results may differ from the reference program's by a relative error of at most 0.006.
Values may be sent and summed in bfloat16 or wider, within the bound.
A program may use at most 64 MiB of HBM per device.

```python
import math
import jax
import jax.numpy as jnp
import numpy as np
from jax import lax

D = 1280
HS = 80
HEADS = 8
P_SIZE = 256
HD = 640
FRAMES = 24
CLIP_MAX = 12
BATCHES = 4
CLIPS = 6


def block_levels(rng, dims, cuts, smallest, top_value):
    gain = 1.0
    for dim, blocks in cuts:
        steps = jax.random.uniform(jax.random.fold_in(jax.random.fold_in(rng, 6), dim), (blocks,), jnp.float32, smallest / len(cuts), top_value / len(cuts))
        gain = gain * jnp.repeat(jnp.exp(steps), dims[dim] // blocks).reshape((-1,) + (1,) * (len(dims) - 1 - dim))
    return gain


def split_up(number_of, total, bound, lean):
    loads = [(1 << 20) // math.isqrt(standing ** lean) + 1 for standing in range(2, number_of + 1)]
    rest, counts = total - bound - (number_of - 1), [1] * (number_of - 1)
    while rest > 0:
        free = [i for i in range(number_of - 1) if counts[i] < bound]
        whole, budget = sum([loads[i] for i in free]), rest
        for i in free:
            more = min(bound - counts[i], max(1, budget * loads[i] // whole), rest)
            counts[i] = counts[i] + more
            rest = rest - more
    return np.array([bound] + counts)


def uneven(rng, count, total, reach, slope):
    if count == 2:
        one = jax.random.randint(rng, (), max(1, total - reach), min(reach, total - 1) + 1)
        return jnp.stack([one, total - one])
    sizes = jnp.asarray(split_up(count, total, reach, slope), jnp.int32)
    pairs = (count - 1) // 2
    donor, receiver = sizes[1:1 + 2 * pairs:2], sizes[2:2 + 2 * pairs:2]
    room = jnp.minimum(donor - 1, reach - receiver)
    passed = jax.random.randint(jax.random.fold_in(rng, 1), (pairs,), 0, 1 << 20) % (room + 1)
    sizes = sizes.at[1:1 + 2 * pairs:2].set(donor - passed).at[2:2 + 2 * pairs:2].set(receiver + passed)
    return sizes[jax.random.permutation(jax.random.fold_in(rng, 2), count)]


def scatter_about(key, extent, scale, limit, shards=(), kind=jnp.bfloat16):
    entries = scale * jax.random.normal(key, extent, jnp.float32)
    if shards:
        entries = entries * block_levels(key, extent, shards, -0.22, 0.18)
    return jnp.clip(entries, -limit, limit).astype(kind)


def setup_inputs(seed: int = 0) -> dict:
    splits = jax.random.split(jax.random.key(seed), 6)
    return {
        "tokens": scatter_about(splits[0], (BATCHES, FRAMES, P_SIZE, D), 1.0, 6.0, ((0, 4), (1, 8))),
        "clip_ids": jax.vmap(lambda own: jnp.searchsorted(jnp.cumsum(uneven(own, CLIPS, FRAMES, CLIP_MAX, 1)), jnp.arange(FRAMES), side="right"))(jax.random.split(splits[1], BATCHES)).reshape((BATCHES, FRAMES)).astype(jnp.int32),
        "ln_gain": jnp.clip(1.0 + 0.18 * jax.random.normal(splits[2], (D,), jnp.float32), 0.1, 1.9),
        "w_qkv": scatter_about(splits[3], (D, 3 * HD), D ** -0.5, 0.15625, ((1, 4),)),
        "w_out": scatter_about(splits[4], (HD, D), HD ** -0.5, 0.25, ((1, 4),)),
    }


norm_eps = 1e-05

def layer_norm(block, ln_gain):
    values = block.astype(jnp.float32)
    center = lax.optimization_barrier(jnp.mean(values, axis=-1, keepdims=True))
    spread = lax.optimization_barrier(jnp.mean(jnp.square(values - center), axis=-1, keepdims=True))
    return ((values - center) * lax.rsqrt(spread + norm_eps) * ln_gain.astype(jnp.float32)).astype(jnp.bfloat16)

def one_batch(inputs, ln_gain, w_qkv, w_out):
    frame_block, clip_row = inputs
    normed = layer_norm(frame_block, ln_gain).reshape(FRAMES * P_SIZE, D)
    projected = jnp.dot(normed, w_qkv, preferred_element_type=jnp.float32)
    queries = (projected[:, :HD] * (1.0 / math.sqrt(HS))).astype(jnp.bfloat16)
    keys = projected[:, HD:2 * HD].astype(jnp.bfloat16)
    values = projected[:, 2 * HD:].astype(jnp.bfloat16)
    head_shape = (FRAMES, P_SIZE, HEADS, HS)
    queries = queries.reshape(head_shape).astype(jnp.float32)
    keys = keys.reshape(head_shape).astype(jnp.float32)
    values = values.reshape(head_shape).astype(jnp.float32)
    scores = jnp.einsum('flhe,glhe->lhfg', queries, keys)
    same_clip = clip_row[:, None] == clip_row[None, :]
    raised = jnp.where(same_clip, jnp.exp(scores), jnp.zeros_like(scores))
    attn_probs = (raised / lax.optimization_barrier(jnp.sum(raised, axis=-1, keepdims=True))).astype(jnp.bfloat16)
    mixed = jnp.einsum('lhfg,glhe->flhe', attn_probs.astype(jnp.float32), values).astype(jnp.bfloat16)
    update = jnp.dot(mixed.reshape(FRAMES * P_SIZE, HD), w_out, preferred_element_type=jnp.float32)
    summed = frame_block.reshape(FRAMES * P_SIZE, D).astype(jnp.float32) + update
    return summed.astype(jnp.bfloat16).reshape(FRAMES, P_SIZE, D)

def reference(tokens, clip_ids, ln_gain, w_qkv, w_out):
    return lax.map(lambda inputs: one_batch(inputs, ln_gain, w_qkv, w_out), (tokens, clip_ids))
```

```python
import functools
import math

import jax
import jax.numpy as jnp
from jax import lax
from jax.experimental import pallas as pl
from jax.experimental.pallas import tpu as pltpu
from jax.sharding import PartitionSpec as P

HS = 80
HEADS = 8
HD = 640
LANES = 128
SUB = 8

norm_eps = 1e-05
MESH = pl.DeviceIdType.MESH
F32, BF16 = jnp.float32, jnp.bfloat16


def kernel(n, ndp, chunks, ch, nb, tokens, w_qkv, w_out, gain, bias, out,
           recv, mix_out, mix_in, wq_st, wq, wo_st, wo, q_s, k_s, v_s, o_s, tok,
           t_send, t_recv, m_send, m_recv, w_send, w_recv, f_send, f_recv, loc):
    me = lax.axis_index("seq")
    dp = lax.axis_index("dp")
    lf, width = tokens.shape[1], tokens.shape[3]
    lp = chunks * ch
    frames = n * lf
    half = ndp // 2
    partner = dp + 1 - 2 * lax.rem(dp, 2)
    groups = ch // SUB

    def peer(k):
        return lax.rem(me + k, n)

    def far(j):
        return lax.rem(dp + 2 * j, ndp)

    barrier = pltpu.get_barrier_semaphore()
    for k in range(1, n):
        pl.semaphore_signal(barrier, inc=1, device_id=(dp, peer(k)), device_id_type=MESH)
    for j in range(1, half):
        pl.semaphore_signal(barrier, inc=1, device_id=(far(j), me), device_id_type=MESH)
    pl.semaphore_signal(barrier, inc=1, device_id=(partner, me), device_id_type=MESH)
    pl.semaphore_wait(barrier, n - 1 + half)

    shards = ((w_qkv, wq_st), (w_out, wo_st))

    def w_copy(which, j):
        source, stage = shards[which]
        target = far(j) if j else partner
        return pltpu.make_async_remote_copy(
            src_ref=source, dst_ref=stage.at[dp],
            send_sem=w_send.at[which, j], recv_sem=w_recv.at[which, j],
            device_id=(target, me), device_id_type=MESH)

    def w_arrived(which, j):
        source, stage = shards[which]
        origin = lax.rem(dp - 2 * j + ndp, ndp) if j else partner
        return pltpu.make_async_remote_copy(
            src_ref=source, dst_ref=stage.at[origin],
            send_sem=w_send.at[which, j], recv_sem=w_recv.at[which, j],
            device_id=(partner, me), device_id_type=MESH)

    def forward(which, j):
        stage = shards[which][1]
        origin = lax.rem(dp - 2 * j + ndp, ndp)
        return pltpu.make_async_remote_copy(
            src_ref=stage.at[origin], dst_ref=stage.at[origin],
            send_sem=f_send.at[which, j], recv_sem=f_recv.at[which, j],
            device_id=(partner, me), device_id_type=MESH)

    def forwarded(which, j):
        stage = shards[which][1]
        origin = lax.rem(partner - 2 * j + ndp, ndp)
        return pltpu.make_async_remote_copy(
            src_ref=stage.at[origin], dst_ref=stage.at[origin],
            send_sem=f_send.at[which, j], recv_sem=f_recv.at[which, j],
            device_id=(partner, me), device_id_type=MESH)

    def rows_of(owner, c):
        return pl.ds(pl.multiple_of(owner * lp + c * ch, SUB), ch)

    def t_copy(c, k):
        return pltpu.make_async_remote_copy(
            src_ref=tokens.at[0, :, rows_of(peer(k), c), :],
            dst_ref=recv.at[c, pl.ds(me * lf, lf)],
            send_sem=t_send.at[c, k], recv_sem=t_recv.at[c, k],
            device_id=(dp, peer(k)), device_id_type=MESH)

    def t_arrived(c, k):
        origin = lax.rem(me - k + n, n)
        return pltpu.make_async_remote_copy(
            src_ref=tokens.at[0, :, rows_of(origin, c), :],
            dst_ref=recv.at[c, pl.ds(origin * lf, lf)],
            send_sem=t_send.at[c, k], recv_sem=t_recv.at[c, k],
            device_id=(dp, origin), device_id_type=MESH)

    def t_own(c):
        return pltpu.make_async_copy(
            tokens.at[0, :, rows_of(me, c), :], recv.at[c, pl.ds(me * lf, lf)], t_recv.at[c, 0])

    def m_copy(c, k):
        return pltpu.make_async_remote_copy(
            src_ref=mix_out.at[c, pl.ds(peer(k) * lf, lf)],
            dst_ref=mix_in.at[c, me],
            send_sem=m_send.at[c, k], recv_sem=m_recv.at[c, k],
            device_id=(dp, peer(k)), device_id_type=MESH)

    def m_arrived(c, k):
        origin = lax.rem(me - k + n, n)
        return pltpu.make_async_remote_copy(
            src_ref=mix_out.at[c, pl.ds(origin * lf, lf)],
            dst_ref=mix_in.at[c, origin],
            send_sem=m_send.at[c, k], recv_sem=m_recv.at[c, k],
            device_id=(dp, origin), device_id_type=MESH)

    def m_own(c):
        return pltpu.make_async_copy(
            mix_out.at[c, pl.ds(me * lf, lf)], mix_in.at[c, me], m_recv.at[c, 0])

    def w_own(which):
        source, stage = shards[which]
        return pltpu.make_async_copy(source, stage.at[dp], loc.at[which])

    for j in range(1, half):
        w_copy(0, j).start()
    for c in range(chunks):
        for k in range(1, n):
            t_copy(c, k).start()
    w_copy(0, 0).start()
    for j in range(half):
        w_copy(1, j).start()
    w_own(0).start()
    w_own(1).start()
    for c in range(chunks):
        t_own(c).start()
    residual = pltpu.make_async_copy(tokens.at[0], tok, loc.at[2])
    residual.start()

    def gather(which, whole):
        stage = shards[which][1]
        for j in range(1, half):
            w_arrived(which, j).wait_recv()
            forward(which, j).start()
        w_own(which).wait()
        w_arrived(which, 0).wait_recv()
        for j in range(1, half):
            forwarded(which, j).wait_recv()
        part = stage.shape[2]
        step = 128

        def place(i, carry):
            rows = pl.ds(pl.multiple_of(i * step, step), step)
            whole[rows, :] = jnp.concatenate([stage[s, rows, :] for s in range(ndp)], axis=1)
            return carry

        lax.fori_loop(0, stage.shape[1] // step, place, 0)

    gather(0, wq)

    block = q_s.shape[1]

    def compute(c, carry):
        t_own(c).wait()
        for k in range(1, n):
            t_arrived(c, k).wait_recv()
        values = recv[c].astype(F32).reshape(frames * ch, width)
        center = jnp.mean(values, axis=-1, keepdims=True)
        moved = values - center
        spread = jnp.mean(jnp.square(moved), axis=-1, keepdims=True)
        normed = (moved * lax.rsqrt(spread + norm_eps) * gain[...]).astype(BF16)

        def split(columns, dest, scale):
            got = jnp.dot(normed, wq[:, columns * HD:(columns + 1) * HD], preferred_element_type=F32)
            if scale is not None:
                got = got * scale
            got = got.reshape(frames, groups, SUB, HD)
            for g in range(groups):
                piece = got[:, g].reshape(frames * SUB, HD).astype(BF16)
                dest[g * (dest.shape[0] // groups):(g + 1) * (dest.shape[0] // groups)] = piece.reshape(
                    dest.shape[0] // groups, dest.shape[1], HD)

        split(0, q_s, 1.0 / math.sqrt(HS))
        split(1, k_s, None)
        split(2, v_s, None)

        def attend(it, inner):
            g = it // nb
            b = lax.rem(it, nb)
            tiles = [None] * (HD // LANES)
            for h in range(HEADS):
                first, last = h * HS, (h + 1) * HS
                lo = first // LANES
                hi = -(-last // LANES)
                cols = slice(lo * LANES, hi * LANES)
                lane = lax.broadcasted_iota(jnp.int32, (block, (hi - lo) * LANES), 1) + lo * LANES
                own = (lane >= first) & (lane < last)
                qh = q_s[it, :, cols].astype(F32)
                qh = jnp.where(own, qh, 0.0).astype(BF16)
                scores = lax.dot_general(
                    qh, k_s[g, :, cols], (((1,), (1,)), ((), ())), preferred_element_type=F32)
                raised = jnp.exp(scores + bias[b])
                probs = (raised / jnp.sum(raised, axis=-1, keepdims=True)).astype(BF16)
                mixed = jnp.dot(probs, v_s[g, :, cols], preferred_element_type=F32)
                for t in range(lo, hi):
                    piece = mixed[:, (t - lo) * LANES:(t - lo + 1) * LANES]
                    if tiles[t] is None:
                        tiles[t] = piece
                    else:
                        inside = own[:, (t - lo) * LANES:(t - lo + 1) * LANES]
                        tiles[t] = jnp.where(inside, piece, tiles[t])
            for t in range(HD // LANES):
                o_s[it, :, t * LANES:(t + 1) * LANES] = tiles[t]
            return inner

        lax.fori_loop(0, groups * nb, attend, 0)
        whole = [o_s[g * nb:(g + 1) * nb].reshape(frames, SUB, HD) for g in range(groups)]
        mix_out[c] = (jnp.concatenate(whole, axis=1) if groups > 1 else whole[0]).astype(BF16)
        for k in range(1, n):
            m_copy(c, k).start()
        m_own(c).start()
        return carry

    lax.fori_loop(0, chunks, compute, 0)
    gather(1, wo)
    residual.wait()

    def finish(c, carry):
        m_own(c).wait()
        for k in range(1, n):
            m_arrived(c, k).wait_recv()
        rows_in = mix_in[c].reshape(n * lf * ch, HD)
        update = jnp.dot(rows_in, wo[...], preferred_element_type=F32).reshape(n, lf, ch, width)
        for s in range(n):
            rows = rows_of(s, c)
            out[0, :, rows, :] = (tok[:, rows, :].astype(F32) + update[s]).astype(BF16)
        return carry

    lax.fori_loop(0, chunks, finish, 0)

    for which in range(2):
        for j in range(half):
            w_copy(which, j).wait_send()
            if j:
                forward(which, j).wait_send()
    for c in range(chunks):
        for k in range(1, n):
            t_copy(c, k).wait_send()
            m_copy(c, k).wait_send()


def shards(n, ndp, tokens, clip_ids, ln_gain, w_qkv, w_out):
    lf, patches, width = tokens.shape[1:]
    frames = n * lf
    lp = patches // n
    ch = 2 * SUB if lp % (2 * SUB) == 0 else SUB
    chunks = lp // ch
    groups = ch // SUB
    rows = frames * SUB
    nb = max(1, rows // 192)
    while rows % nb or (rows // nb) % (2 * SUB):
        nb -= 1
    block = rows // nb
    clip = clip_ids[0]
    lowest = float(jnp.finfo(F32).min)
    place = clip[:, None] * SUB + jnp.arange(SUB, dtype=jnp.int32)[None, :]
    place = place.reshape(rows)
    bias = jnp.where(place[:, None] == place[None, :], 0.0, lowest).astype(F32).reshape(nb, block, rows)
    qcols, ocols = w_qkv.shape[1], w_out.shape[1]
    half = ndp // 2
    vm, dma = pltpu.VMEM, pltpu.SemaphoreType.DMA
    whole = pl.BlockSpec(memory_space=pltpu.VMEM)
    away = pl.BlockSpec(memory_space=pl.ANY)
    return pl.pallas_call(
        functools.partial(kernel, n, ndp, chunks, ch, nb),
        out_shape=jax.ShapeDtypeStruct(tokens.shape, BF16),
        in_specs=[away, away, away, whole, whole],
        out_specs=whole,
        scratch_shapes=[
            vm((chunks, frames, ch, width), BF16),
            vm((chunks, frames, ch, HD), BF16),
            vm((chunks, n, lf, ch, HD), BF16),
            vm((ndp, width, qcols), BF16),
            vm((width, 3 * HD), BF16),
            vm((ndp, HD, ocols), BF16),
            vm((HD, width), BF16),
            vm((groups * nb, block, HD), BF16),
            vm((groups, rows, HD), BF16),
            vm((groups, rows, HD), BF16),
            vm((groups * nb, block, HD), F32),
            vm((lf, patches, width), BF16),
            dma((chunks, n)), dma((chunks, n)), dma((chunks, n)), dma((chunks, n)),
            dma((2, half)), dma((2, half)), dma((2, half)), dma((2, half)), dma((3,)),
        ],
        compiler_params=pltpu.CompilerParams(
            collective_id=0, has_side_effects=True, vmem_limit_bytes=60 * 1024 * 1024),
    )(tokens, w_qkv, w_out, ln_gain.astype(F32).reshape(1, width), bias)


def solution(mesh):
    placed = (P("dp", "seq", None, None), P("dp", None), P(), P(None, "dp"), P(None, "dp"))
    return jax.shard_map(
        functools.partial(shards, mesh.shape["seq"], mesh.shape["dp"]),
        mesh=mesh, in_specs=placed, out_specs=P("dp", "seq", None, None), check_vma=False)
```

```python
import functools
import math

import jax
import jax.numpy as jnp
from jax import lax
from jax.experimental import pallas as pl
from jax.experimental.pallas import tpu as pltpu
from jax.sharding import PartitionSpec as P

HS = 80
HEADS = 8
HD = 640
LANES = 128
SUB = 8

norm_eps = 1e-05
MESH = pl.DeviceIdType.MESH
F32, BF16 = jnp.float32, jnp.bfloat16


def kernel(n, ndp, chunks, ch, nb, tokens, w_qkv, w_out, gain, clip, out,
           recv, mix_out, mix_in, wq_st, wq, wo_st, wo, q_s, k_s, v_s, o_s, bias, tok,
           t_send, t_recv, m_send, m_recv, w_send, w_recv, f_send, f_recv, loc):
    me = lax.axis_index("seq")
    dp = lax.axis_index("dp")
    lf, width = tokens.shape[1], tokens.shape[3]
    lp = chunks * ch
    frames = n * lf
    half = ndp // 2
    partner = dp + 1 - 2 * lax.rem(dp, 2)
    groups = ch // SUB

    def peer(k):
        if n & (n - 1):
            return lax.rem(me + k, n)
        other = me
        bit = 1
        while bit < n:
            if k & bit:
                other = other + bit - 2 * bit * lax.rem(me // bit, 2)
            bit *= 2
        return other

    def source_of(k):
        return lax.rem(me - k + n, n) if n & (n - 1) else peer(k)

    order = range(n - 1, 0, -1)

    def far(j):
        return lax.rem(dp + 2 * j, ndp)

    barrier = pltpu.get_barrier_semaphore()
    for k in order:
        pl.semaphore_signal(barrier, inc=1, device_id=(dp, peer(k)), device_id_type=MESH)
    for j in range(1, half):
        pl.semaphore_signal(barrier, inc=1, device_id=(far(j), me), device_id_type=MESH)
    pl.semaphore_signal(barrier, inc=1, device_id=(partner, me), device_id_type=MESH)
    pl.semaphore_wait(barrier, n - 1 + half)

    shards = ((w_qkv, wq_st, wq), (w_out, wo_st, wo))

    def slot(which, owner):
        source, stage, whole = shards[which]
        part = source.shape[0]
        if part % (2 * SUB):
            return stage.at[owner]
        return whole.at[pl.ds(pl.multiple_of(owner * part, 2 * SUB), part)]

    def w_move(which, j, source, owner, target, send, arrive):
        return pltpu.make_async_remote_copy(
            src_ref=source, dst_ref=slot(which, owner),
            send_sem=send.at[which, j], recv_sem=arrive.at[which, j],
            device_id=(target, me), device_id_type=MESH)

    def w_copy(which, j):
        return w_move(which, j, shards[which][0], dp, far(j) if j else partner, w_send, w_recv)

    def w_arrived(which, j):
        origin = lax.rem(dp - 2 * j + ndp, ndp) if j else partner
        return w_move(which, j, shards[which][0], origin, partner, w_send, w_recv)

    def forward(which, j):
        origin = lax.rem(dp - 2 * j + ndp, ndp)
        return w_move(which, j, slot(which, origin), origin, partner, f_send, f_recv)

    def forwarded(which, j):
        origin = lax.rem(partner - 2 * j + ndp, ndp)
        return w_move(which, j, slot(which, origin), origin, partner, f_send, f_recv)

    def rows_of(owner, c):
        return pl.ds(pl.multiple_of(owner * lp + c * ch, SUB), ch)

    def t_copy(c, k):
        return pltpu.make_async_remote_copy(
            src_ref=tokens.at[0, :, rows_of(peer(k), c), :],
            dst_ref=recv.at[c, pl.ds(me * lf, lf)],
            send_sem=t_send.at[c, k], recv_sem=t_recv.at[c, k],
            device_id=(dp, peer(k)), device_id_type=MESH)

    def t_arrived(c, k):
        origin = source_of(k)
        return pltpu.make_async_remote_copy(
            src_ref=tokens.at[0, :, rows_of(origin, c), :],
            dst_ref=recv.at[c, pl.ds(origin * lf, lf)],
            send_sem=t_send.at[c, k], recv_sem=t_recv.at[c, k],
            device_id=(dp, origin), device_id_type=MESH)

    def t_own(c):
        return pltpu.make_async_copy(
            tokens.at[0, :, rows_of(me, c), :], recv.at[c, pl.ds(me * lf, lf)], t_recv.at[c, 0])

    def m_copy(c, k):
        return pltpu.make_async_remote_copy(
            src_ref=mix_out.at[c, pl.ds(peer(k) * lf, lf)],
            dst_ref=mix_in.at[c, me],
            send_sem=m_send.at[c, k], recv_sem=m_recv.at[c, k],
            device_id=(dp, peer(k)), device_id_type=MESH)

    def m_arrived(c, k):
        origin = source_of(k)
        return pltpu.make_async_remote_copy(
            src_ref=mix_out.at[c, pl.ds(origin * lf, lf)],
            dst_ref=mix_in.at[c, origin],
            send_sem=m_send.at[c, k], recv_sem=m_recv.at[c, k],
            device_id=(dp, origin), device_id_type=MESH)

    def m_own(c):
        return pltpu.make_async_copy(
            mix_out.at[c, pl.ds(me * lf, lf)], mix_in.at[c, me], m_recv.at[c, 0])

    def w_own(which):
        return pltpu.make_async_copy(shards[which][0], slot(which, dp), loc.at[which])

    for j in range(1, half):
        w_copy(0, j).start()
    for c in range(chunks):
        for k in order:
            t_copy(c, k).start()
    w_copy(0, 0).start()
    for j in range(half):
        w_copy(1, j).start()
    w_own(0).start()
    w_own(1).start()
    for c in range(chunks):
        t_own(c).start()
    residual = pltpu.make_async_copy(tokens.at[0], tok, loc.at[2])
    residual.start()

    def gather(which):
        source, stage, whole = shards[which]
        for j in range(1, half):
            w_arrived(which, j).wait_recv()
            forward(which, j).start()
        w_own(which).wait()
        w_arrived(which, 0).wait_recv()
        for j in range(1, half):
            forwarded(which, j).wait_recv()
        part = source.shape[0]
        if part % (2 * SUB):
            for owner in range(ndp):
                whole[owner * part:(owner + 1) * part, :] = stage[owner]

    frames_of = lax.broadcasted_iota(jnp.int32, (frames * SUB, 1), 0)
    along = lax.broadcasted_iota(jnp.int32, (1, frames * SUB), 1)

    def name(f, carry):
        down, across = carry
        return (jnp.where(frames_of // SUB == f, clip[0, f], down),
                jnp.where(along // SUB == f, clip[0, f], across))

    down, across = lax.fori_loop(
        0, frames, name, (jnp.zeros_like(frames_of), jnp.zeros_like(along)))
    same = (down * SUB + frames_of % SUB) == (across * SUB + along % SUB)
    bias[...] = jnp.where(same, 0.0, float(jnp.finfo(F32).min)).reshape(bias.shape)

    gather(0)

    block = q_s.shape[1]

    def compute(c, carry):
        t_own(c).wait()
        for k in order:
            t_arrived(c, k).wait_recv()
        values = recv[c].astype(F32).reshape(frames * ch, width)
        center = jnp.mean(values, axis=-1, keepdims=True)
        moved = values - center
        spread = jnp.mean(jnp.square(moved), axis=-1, keepdims=True)
        normed = (moved * lax.rsqrt(spread + norm_eps) * gain[...].reshape(1, width)).astype(BF16)

        def split(columns, dest, scale):
            got = lax.dot_general(
                normed, wq[columns * HD:(columns + 1) * HD, :], (((1,), (1,)), ((), ())), preferred_element_type=F32)
            if scale is not None:
                got = got * scale
            got = got.reshape(frames, groups, SUB, HD)
            for g in range(groups):
                piece = got[:, g].reshape(frames * SUB, HD).astype(BF16)
                dest[g * (dest.shape[0] // groups):(g + 1) * (dest.shape[0] // groups)] = piece.reshape(
                    dest.shape[0] // groups, dest.shape[1], HD)

        split(0, q_s, 1.0 / math.sqrt(HS))
        split(1, k_s, None)
        split(2, v_s, None)

        def attend(it, inner):
            g = it // nb
            b = lax.rem(it, nb)
            tiles = [None] * (HD // LANES)
            for h in range(HEADS):
                first, last = h * HS, (h + 1) * HS
                lo = first // LANES
                hi = -(-last // LANES)
                cols = slice(lo * LANES, hi * LANES)
                lane = lax.broadcasted_iota(jnp.int32, (block, (hi - lo) * LANES), 1) + lo * LANES
                own = (lane >= first) & (lane < last)
                qh = q_s[it, :, cols].astype(F32)
                qh = jnp.where(own, qh, 0.0).astype(BF16)
                scores = lax.dot_general(
                    qh, k_s[g, :, cols], (((1,), (1,)), ((), ())), preferred_element_type=F32)
                raised = jnp.exp(scores + bias[b])
                probs = (raised / jnp.sum(raised, axis=-1, keepdims=True)).astype(BF16)
                mixed = jnp.dot(probs, v_s[g, :, cols], preferred_element_type=F32)
                for t in range(lo, hi):
                    piece = mixed[:, (t - lo) * LANES:(t - lo + 1) * LANES]
                    if tiles[t] is None:
                        tiles[t] = piece
                    else:
                        inside = own[:, (t - lo) * LANES:(t - lo + 1) * LANES]
                        tiles[t] = jnp.where(inside, piece, tiles[t])
            for t in range(HD // LANES):
                o_s[it, :, t * LANES:(t + 1) * LANES] = tiles[t]
            return inner

        lax.fori_loop(0, groups * nb, attend, 0)
        whole = [o_s[g * nb:(g + 1) * nb].reshape(frames, SUB, HD) for g in range(groups)]
        mix_out[c] = (jnp.concatenate(whole, axis=1) if groups > 1 else whole[0]).astype(BF16)
        for k in order:
            m_copy(c, k).start()
        m_own(c).start()
        return carry

    lax.fori_loop(0, chunks, compute, 0)
    gather(1)
    residual.wait()

    def finish(c, carry):
        m_own(c).wait()
        for k in order:
            m_arrived(c, k).wait_recv()
        rows_in = mix_in[c].reshape(n * lf * ch, HD)
        update = lax.dot_general(
            rows_in, wo[...], (((1,), (1,)), ((), ())), preferred_element_type=F32).reshape(n, lf, ch, width)
        for s in range(n):
            rows = rows_of(s, c)
            out[0, :, rows, :] = (tok[:, rows, :].astype(F32) + update[s]).astype(BF16)
        return carry

    lax.fori_loop(0, chunks, finish, 0)

    for which in range(2):
        for j in range(half):
            w_copy(which, j).wait_send()
            if j:
                forward(which, j).wait_send()
    for c in range(chunks):
        for k in order:
            t_copy(c, k).wait_send()
            m_copy(c, k).wait_send()


def shards(n, ndp, tokens, clip_ids, ln_gain, w_qkv, w_out):
    lf, patches, width = tokens.shape[1:]
    frames = n * lf
    lp = patches // n
    ch = 2 * SUB if lp % (2 * SUB) == 0 else SUB
    chunks = lp // ch
    groups = ch // SUB
    rows = frames * SUB
    nb = max(1, rows // 192)
    while rows % nb or (rows // nb) % (2 * SUB):
        nb -= 1
    block = rows // nb
    qcols, ocols = w_qkv.shape[1], w_out.shape[1]
    half = ndp // 2
    vm, dma = pltpu.VMEM, pltpu.SemaphoreType.DMA

    def staged(columns, depth):
        return vm((ndp, columns, depth) if columns % (2 * SUB) else (1, 2 * SUB, LANES), BF16)

    whole = pl.BlockSpec(memory_space=pltpu.VMEM)
    away = pl.BlockSpec(memory_space=pl.ANY)
    return pl.pallas_call(
        functools.partial(kernel, n, ndp, chunks, ch, nb),
        out_shape=jax.ShapeDtypeStruct(tokens.shape, BF16),
        in_specs=[away, away, away, whole, pl.BlockSpec(memory_space=pltpu.SMEM)],
        out_specs=whole,
        scratch_shapes=[
            vm((chunks, frames, ch, width), BF16),
            vm((chunks, frames, ch, HD), BF16),
            vm((chunks, n, lf, ch, HD), BF16),
            staged(qcols, width),
            vm((3 * HD, width), BF16),
            staged(ocols, HD),
            vm((width, HD), BF16),
            vm((groups * nb, block, HD), BF16),
            vm((groups, rows, HD), BF16),
            vm((groups, rows, HD), BF16),
            vm((groups * nb, block, HD), F32),
            vm((nb, block, rows), F32),
            vm((lf, patches, width), BF16),
            dma((chunks, n)), dma((chunks, n)), dma((chunks, n)), dma((chunks, n)),
            dma((2, half)), dma((2, half)), dma((2, half)), dma((2, half)), dma((3,)),
        ],
        compiler_params=pltpu.CompilerParams(
            collective_id=0, has_side_effects=True, vmem_limit_bytes=60 * 1024 * 1024),
    )(tokens, w_qkv.T, w_out.T, ln_gain, clip_ids)


def solution(mesh):
    placed = (P("dp", "seq", None, None), P("dp", None), P(), P(None, "dp"), P(None, "dp"))
    return jax.shard_map(
        functools.partial(shards, mesh.shape["seq"], mesh.shape["dp"]),
        mesh=mesh, in_specs=placed, out_specs=P("dp", "seq", None, None), check_vma=False)
```

```python
import functools
import math

import jax
import jax.numpy as jnp
from jax import lax
from jax.experimental import pallas as pl
from jax.experimental.pallas import tpu as pltpu
from jax.sharding import PartitionSpec as P

HS = 80
HEADS = 8
HD = 640
LANES = 128
SUB = 8

norm_eps = 1e-05
MESH = pl.DeviceIdType.MESH
F32, BF16 = jnp.float32, jnp.bfloat16


def kernel(n, ndp, chunks, ch, nb, tokens, w_qkv, w_out, gain, clip, out,
           recv, mix_out, mix_in, wq_st, wq, wo_st, wo, q_s, k_s, v_s, o_s, bias, tok,
           t_send, t_recv, m_send, m_recv, w_send, w_recv, f_send, f_recv, loc):
    me = lax.axis_index("seq")
    dp = lax.axis_index("dp")
    lf, width = tokens.shape[1], tokens.shape[3]
    lp = chunks * ch
    frames = n * lf
    half = ndp // 2
    partner = dp + 1 - 2 * lax.rem(dp, 2)
    groups = ch // SUB

    def peer(k):
        if n & (n - 1):
            return lax.rem(me + k, n)
        other = me
        bit = 1
        while bit < n:
            if k & bit:
                other = other + bit - 2 * bit * lax.rem(me // bit, 2)
            bit *= 2
        return other

    def source_of(k):
        return lax.rem(me - k + n, n) if n & (n - 1) else peer(k)

    order = range(n - 1, 0, -1)

    def far(j):
        return lax.rem(dp + 2 * j, ndp)

    barrier = pltpu.get_barrier_semaphore()
    for k in order:
        pl.semaphore_signal(barrier, inc=1, device_id=(dp, peer(k)), device_id_type=MESH)
    for j in range(1, half):
        pl.semaphore_signal(barrier, inc=1, device_id=(far(j), me), device_id_type=MESH)
    pl.semaphore_signal(barrier, inc=1, device_id=(partner, me), device_id_type=MESH)
    pl.semaphore_wait(barrier, n - 1 + half)

    shards = ((w_qkv, wq_st, wq), (w_out, wo_st, wo))

    def slot(which, owner):
        source, stage, whole = shards[which]
        part = source.shape[0]
        if part % (2 * SUB):
            return stage.at[owner]
        return whole.at[pl.ds(pl.multiple_of(owner * part, 2 * SUB), part)]

    def w_move(which, j, source, owner, target, send, arrive):
        return pltpu.make_async_remote_copy(
            src_ref=source, dst_ref=slot(which, owner),
            send_sem=send.at[which, j], recv_sem=arrive.at[which, j],
            device_id=(target, me), device_id_type=MESH)

    def w_copy(which, j):
        return w_move(which, j, shards[which][0], dp, far(j) if j else partner, w_send, w_recv)

    def w_arrived(which, j):
        origin = lax.rem(dp - 2 * j + ndp, ndp) if j else partner
        return w_move(which, j, shards[which][0], origin, partner, w_send, w_recv)

    def forward(which, j):
        origin = lax.rem(dp - 2 * j + ndp, ndp)
        return w_move(which, j, slot(which, origin), origin, partner, f_send, f_recv)

    def forwarded(which, j):
        origin = lax.rem(partner - 2 * j + ndp, ndp)
        return w_move(which, j, slot(which, origin), origin, partner, f_send, f_recv)

    def rows_of(owner, c):
        return pl.ds(pl.multiple_of(owner * lp + c * ch, SUB), ch)

    def t_copy(c, k):
        return pltpu.make_async_remote_copy(
            src_ref=tokens.at[0, :, rows_of(peer(k), c), :],
            dst_ref=recv.at[c, pl.ds(me * lf, lf)],
            send_sem=t_send.at[c, k], recv_sem=t_recv.at[c, k],
            device_id=(dp, peer(k)), device_id_type=MESH)

    def t_arrived(c, k):
        origin = source_of(k)
        return pltpu.make_async_remote_copy(
            src_ref=tokens.at[0, :, rows_of(origin, c), :],
            dst_ref=recv.at[c, pl.ds(origin * lf, lf)],
            send_sem=t_send.at[c, k], recv_sem=t_recv.at[c, k],
            device_id=(dp, origin), device_id_type=MESH)

    def t_own(c):
        return pltpu.make_async_copy(
            tokens.at[0, :, rows_of(me, c), :], recv.at[c, pl.ds(me * lf, lf)], t_recv.at[c, 0])

    def m_copy(c, k):
        return pltpu.make_async_remote_copy(
            src_ref=mix_out.at[c, pl.ds(peer(k) * lf, lf)],
            dst_ref=mix_in.at[c, me],
            send_sem=m_send.at[c, k], recv_sem=m_recv.at[c, k],
            device_id=(dp, peer(k)), device_id_type=MESH)

    def m_arrived(c, k):
        origin = source_of(k)
        return pltpu.make_async_remote_copy(
            src_ref=mix_out.at[c, pl.ds(origin * lf, lf)],
            dst_ref=mix_in.at[c, origin],
            send_sem=m_send.at[c, k], recv_sem=m_recv.at[c, k],
            device_id=(dp, origin), device_id_type=MESH)

    def m_own(c):
        return pltpu.make_async_copy(
            mix_out.at[c, pl.ds(me * lf, lf)], mix_in.at[c, me], m_recv.at[c, 0])

    def w_own(which):
        return pltpu.make_async_copy(shards[which][0], slot(which, dp), loc.at[which])

    for j in range(1, half):
        w_copy(0, j).start()
    for c in range(chunks):
        for k in order:
            t_copy(c, k).start()
    w_copy(0, 0).start()
    for j in range(half):
        w_copy(1, j).start()
    w_own(0).start()
    w_own(1).start()
    for c in range(chunks):
        t_own(c).start()
    residual = pltpu.make_async_copy(tokens.at[0], tok, loc.at[2])
    residual.start()

    def gather(which):
        source, stage, whole = shards[which]
        for j in range(1, half):
            w_arrived(which, j).wait_recv()
            forward(which, j).start()
        w_own(which).wait()
        w_arrived(which, 0).wait_recv()
        for j in range(1, half):
            forwarded(which, j).wait_recv()
        part = source.shape[0]
        if part % (2 * SUB):
            for owner in range(ndp):
                whole[owner * part:(owner + 1) * part, :] = stage[owner]

    frames_of = lax.broadcasted_iota(jnp.int32, (frames * SUB, 1), 0)
    along = lax.broadcasted_iota(jnp.int32, (1, frames * SUB), 1)

    def name(f, carry):
        down, across = carry
        return (jnp.where(frames_of // SUB == f, clip[0, f], down),
                jnp.where(along // SUB == f, clip[0, f], across))

    down, across = lax.fori_loop(
        0, frames, name, (jnp.zeros_like(frames_of), jnp.zeros_like(along)))
    same = (down * SUB + frames_of % SUB) == (across * SUB + along % SUB)
    bias[...] = jnp.where(same, 0.0, float(jnp.finfo(F32).min)).reshape(bias.shape)

    gather(0)

    block = q_s.shape[1]

    def compute(c, carry):
        t_own(c).wait()
        for k in order:
            t_arrived(c, k).wait_recv()
        values = recv[c].astype(F32).reshape(frames * ch, width)
        center = jnp.mean(values, axis=-1, keepdims=True)
        moved = values - center
        spread = jnp.mean(jnp.square(moved), axis=-1, keepdims=True)
        normed = (moved * lax.rsqrt(spread + norm_eps) * gain[...].reshape(1, width)).astype(BF16)

        def split(columns, dest, scale):
            got = lax.dot_general(
                normed, wq[columns * HD:(columns + 1) * HD, :], (((1,), (1,)), ((), ())), preferred_element_type=F32)
            if scale is not None:
                got = got * scale
            got = got.reshape(frames, groups, SUB, HD)
            for g in range(groups):
                piece = got[:, g].reshape(frames * SUB, HD).astype(BF16)
                dest[g * (dest.shape[0] // groups):(g + 1) * (dest.shape[0] // groups)] = piece.reshape(
                    dest.shape[0] // groups, dest.shape[1], HD)

        split(0, q_s, 1.0 / math.sqrt(HS))
        split(1, k_s, None)
        split(2, v_s, None)

        def attend(it, inner):
            g = it // nb
            b = lax.rem(it, nb)
            tiles = [None] * (HD // LANES)
            for h in range(HEADS):
                first, last = h * HS, (h + 1) * HS
                lo = first // LANES
                hi = -(-last // LANES)
                cols = slice(lo * LANES, hi * LANES)
                lane = lax.broadcasted_iota(jnp.int32, (block, (hi - lo) * LANES), 1) + lo * LANES
                own = (lane >= first) & (lane < last)
                qh = q_s[it, :, cols].astype(F32)
                qh = jnp.where(own, qh, 0.0).astype(BF16)
                scores = lax.dot_general(
                    qh, k_s[g, :, cols], (((1,), (1,)), ((), ())), preferred_element_type=F32)
                raised = jnp.exp(scores + bias[b])
                probs = (raised / jnp.sum(raised, axis=-1, keepdims=True)).astype(BF16)
                mixed = jnp.dot(probs, v_s[g, :, cols], preferred_element_type=F32)
                for t in range(lo, hi):
                    piece = mixed[:, (t - lo) * LANES:(t - lo + 1) * LANES]
                    if tiles[t] is None:
                        tiles[t] = piece
                    else:
                        inside = own[:, (t - lo) * LANES:(t - lo + 1) * LANES]
                        tiles[t] = jnp.where(inside, piece, tiles[t])
            for t in range(HD // LANES):
                o_s[it, :, t * LANES:(t + 1) * LANES] = tiles[t]
            return inner

        lax.fori_loop(0, groups * nb, attend, 0)
        whole = [o_s[g * nb:(g + 1) * nb].reshape(frames, SUB, HD) for g in range(groups)]
        mix_out[c] = (jnp.concatenate(whole, axis=1) if groups > 1 else whole[0]).astype(BF16)
        for k in order:
            m_copy(c, k).start()
        m_own(c).start()
        return carry

    lax.fori_loop(0, chunks, compute, 0)
    gather(1)
    residual.wait()

    def finish(c, carry):
        m_own(c).wait()
        for k in order:
            m_arrived(c, k).wait_recv()
        rows_in = mix_in[c].reshape(n * lf * ch, HD)
        update = lax.dot_general(
            rows_in, wo[...], (((1,), (1,)), ((), ())), preferred_element_type=F32).reshape(n, lf, ch, width)
        for s in range(n):
            rows = rows_of(s, c)
            out[0, :, rows, :] = (tok[:, rows, :].astype(F32) + update[s]).astype(BF16)
        return carry

    lax.fori_loop(0, chunks, finish, 0)

    for which in range(2):
        for j in range(half):
            w_copy(which, j).wait_send()
            if j:
                forward(which, j).wait_send()
    for c in range(chunks):
        for k in order:
            t_copy(c, k).wait_send()
            m_copy(c, k).wait_send()


def shards(n, ndp, tokens, clip_ids, ln_gain, w_qkv, w_out):
    lf, patches, width = tokens.shape[1:]
    frames = n * lf
    lp = patches // n
    ch = 2 * SUB if lp % (2 * SUB) == 0 else SUB
    chunks = lp // ch
    groups = ch // SUB
    rows = frames * SUB
    nb = max(1, rows // 192)
    while rows % nb or (rows // nb) % (2 * SUB):
        nb -= 1
    block = rows // nb
    qcols, ocols = w_qkv.shape[1], w_out.shape[1]
    half = ndp // 2
    vm, dma = pltpu.VMEM, pltpu.SemaphoreType.DMA

    def staged(columns, depth):
        return vm((ndp, columns, depth) if columns % (2 * SUB) else (1, 2 * SUB, LANES), BF16)

    whole = pl.BlockSpec(memory_space=pltpu.VMEM)
    away = pl.BlockSpec(memory_space=pl.ANY)
    return pl.pallas_call(
        functools.partial(kernel, n, ndp, chunks, ch, nb),
        out_shape=pltpu.VMEM(tokens.shape, BF16),
        in_specs=[away, away, away, whole, pl.BlockSpec(memory_space=pltpu.SMEM)],
        out_specs=whole,
        scratch_shapes=[
            vm((chunks, frames, ch, width), BF16),
            vm((chunks, frames, ch, HD), BF16),
            vm((chunks, n, lf, ch, HD), BF16),
            staged(qcols, width),
            vm((3 * HD, width), BF16),
            staged(ocols, HD),
            vm((width, HD), BF16),
            vm((groups * nb, block, HD), BF16),
            vm((groups, rows, HD), BF16),
            vm((groups, rows, HD), BF16),
            vm((groups * nb, block, HD), F32),
            vm((nb, block, rows), F32),
            vm((lf, patches, width), BF16),
            dma((chunks, n)), dma((chunks, n)), dma((chunks, n)), dma((chunks, n)),
            dma((2, half)), dma((2, half)), dma((2, half)), dma((2, half)), dma((3,)),
        ],
        compiler_params=pltpu.CompilerParams(
            collective_id=0, has_side_effects=True, vmem_limit_bytes=60 * 1024 * 1024),
    )(tokens, w_qkv.T, w_out.T, ln_gain, clip_ids)


def solution(mesh):
    placed = (P("dp", "seq", None, None), P("dp", None), P(), P(None, "dp"), P(None, "dp"))
    return jax.shard_map(
        functools.partial(shards, mesh.shape["seq"], mesh.shape["dp"]),
        mesh=mesh, in_specs=placed, out_specs=P("dp", "seq", None, None), check_vma=False)
```
